32 devices in a mesh: seq: 8 (over y, x, core), fsdp: 4 (over z).
Axes of the slice: x: 2, y: 2, z: 4, core: 2. Of those that a mesh axis runs over, the one named last changes fastest.
Arguments:
- hidden_in: bfloat16 [4, 1024, 2304], P('fsdp', 'seq'), may hold values from -6 to 6
- qkv_weights: bfloat16 [2304, 4096], P(('seq', 'fsdp')), may hold values from -0.375 to 0.375
- out_weights: bfloat16 [2304, 2048], P(('seq', 'fsdp')), may hold values from -0.125 to 0.125
- gate_up_weights: bfloat16 [2304, 18432], P(('seq', 'fsdp')), may hold values from -0.125 to 0.125
- down_weights: bfloat16 [2304, 9216], P(('seq', 'fsdp')), may hold values from -0.0625 to 0.0625
- norm_gains: bfloat16 [4, 2304], P(None, ('seq', 'fsdp')), may hold values from -0.5 to 0.5
- doc_ids: int32 [4, 1024], P('fsdp', 'seq'), may hold values from 0 to 2, never falling along the last dimension, each value on 1 to 768 neighbouring positions
- cotangent: bfloat16 [4, 1024, 2304], P('fsdp', 'seq'), may hold values from -6 to 6
Outputs:
- hidden_out: bfloat16 [4, 1024, 2304], P('fsdp', 'seq')
- hidden_grad: float32 [4, 1024, 2304], P('fsdp', 'seq')
- qkv_grad: float32 [2304, 4096], P(('seq', 'fsdp'))
- out_grad: float32 [2304, 2048], P(('seq', 'fsdp'))
- gate_up_grad: float32 [2304, 18432], P(('seq', 'fsdp'))
- down_grad: float32 [2304, 9216], P(('seq', 'fsdp'))
- gain_grad: float32 [4, 2304], P(None, ('seq', 'fsdp'))
The draws below stay inside these ranges and needn't reach their ends.
Inputs may be any that keep to these rules, and one draw needn't show every extreme that they name: `doc_ids`: in each pack the ids never fall, each of the 3 documents holds one token or more, and the longest holds exactly 768.
All inputs are finite; a program needn't handle non-finite values.
Results may differ from the reference program's by a relative error of at most 0.028.
The reference program's roundings to bfloat16 on the way count: a program that leaves them out, or rounds other values in their place, can miss the bound.
Values may be sent and summed in bfloat16 or wider, within the bound.
No kernel may reach another device: no remote copies, remote signals or barrier semaphores. Data moves between devices by JAX's collectives and lax.ppermute only.
A program may use at most 384 MiB of HBM per device.

```python
import math
import jax
import jax.numpy as jnp
import numpy as np
from jax import lax

D = 2304
HEADS = 8
KV_HEADS = 4
HEAD_DIM = 256
FF = 9216
DOCS = 3
SEQ_LEN = 1024
PACKS = 4


def raised(drawn, rng, source, target, blocks, factor):
    def block_of(axis_at):
        return (jnp.arange(drawn.shape[axis_at]) // (drawn.shape[axis_at] // blocks)).reshape((-1,) + (1,) * (drawn.ndim - 1 - axis_at))

    first = jax.random.permutation(rng, blocks)[block_of(target)]
    other_side = (block_of(target) + blocks // 2) % blocks
    return jnp.where((block_of(source) == first) | (block_of(source) == other_side), factor * drawn, drawn)


def level_of(stream_key, dims, shards, low, largest):
    gain, own = 1.0, jax.random.fold_in(stream_key, 6)
    for axis_at, shards_of in shards:
        draws = jnp.exp(jax.random.uniform(jax.random.fold_in(own, axis_at), (shards_of,), jnp.float32, low / len(shards), largest / len(shards)))
        gain = gain * jnp.repeat(draws, dims[axis_at] // shards_of).reshape([-1 if axis == axis_at else 1 for axis in range(len(dims))])
    return gain


def length_profile(number_of, total, limit, skew):
    portions = [(1 << 20) // math.isqrt(rank ** skew) + 1 for rank in range(2, number_of + 1)]
    surplus, given = total - limit - (number_of - 1), [1] * (number_of - 1)
    while surplus > 0:
        free = [i for i in range(number_of - 1) if given[i] < limit]
        pool, left = sum([portions[i] for i in free]), surplus
        for i in free:
            extra = min(limit - given[i], max(1, left * portions[i] // pool), surplus)
            given[i] = given[i] + extra
            surplus = surplus - extra
    return np.array([limit] + given)


def ragged(rng, amount, total, limit, lean):
    if amount == 2:
        one = jax.random.randint(rng, (), max(1, total - limit), min(limit, total - 1) + 1)
        return jnp.stack([one, total - one])
    lengths = jnp.asarray(length_profile(amount, total, limit, lean), jnp.int32)
    pairs = (amount - 1) // 2
    giver, sink = lengths[1:1 + 2 * pairs:2], lengths[2:2 + 2 * pairs:2]
    slack = jnp.minimum(giver - 1, limit - sink)
    passed = jax.random.randint(jax.random.fold_in(rng, 1), (pairs,), 0, 1 << 20) % (slack + 1)
    lengths = lengths.at[1:1 + 2 * pairs:2].set(giver - passed).at[2:2 + 2 * pairs:2].set(sink + passed)
    return lengths[jax.random.permutation(jax.random.fold_in(rng, 2), amount)]


def noise(stream_key, shape, scale, bound, pieces=(), kind=jnp.bfloat16):
    values = scale * jax.random.normal(stream_key, shape, jnp.float32)
    if pieces:
        values = values * level_of(stream_key, shape, pieces, -0.22, 0.18)
    return jnp.clip(values, -bound, bound).astype(kind)


def bell_draw_with(own_key, dims, scale, reach, cuts, heavy, kind=jnp.bfloat16):
    array = scale * jax.random.normal(own_key, dims, jnp.float32)
    if cuts:
        array = array * level_of(own_key, dims, cuts, -0.22, 0.18)
    return jnp.clip(raised(array, jax.random.fold_in(own_key, 3), *heavy), -reach, reach).astype(kind)


def setup_inputs(seed: int = 0) -> dict:
    arg_keys = jax.random.split(jax.random.key(seed), 9)
    return {
        "hidden_in": noise(arg_keys[0], (PACKS, SEQ_LEN, D), 1.0, 6.0, ((0, 4), (1, 8))),
        "qkv_weights": noise(arg_keys[1], (D, (HEADS + 2 * KV_HEADS) * HEAD_DIM), (D // 8) ** -0.5, 0.375, ((0, 32),)),
        "out_weights": noise(arg_keys[2], (D, HEADS * HEAD_DIM), (HEADS * HEAD_DIM) ** -0.5, 0.125, ((0, 32),)),
        "gate_up_weights": noise(arg_keys[3], (D, 2 * FF), D ** -0.5, 0.125, ((0, 32),)),
        "down_weights": noise(arg_keys[4], (D, FF), FF ** -0.5, 0.0625, ((0, 32),)),
        "norm_gains": jnp.clip(jax.random.uniform(arg_keys[5], (4, D), jnp.float32, -0.5, 0.5) * level_of(arg_keys[5], (4, D), ((1, 32),), -0.4, 0.0), -0.5, 0.5).astype(jnp.bfloat16),
        "doc_ids": jax.vmap(lambda own: jnp.searchsorted(jnp.cumsum(ragged(own, DOCS, SEQ_LEN, 3 * SEQ_LEN // 4, 0)), jnp.arange(SEQ_LEN), side="right"))(jax.random.split(arg_keys[6], PACKS)).reshape((PACKS, SEQ_LEN)).astype(jnp.int32),
        "cotangent": bell_draw_with(arg_keys[7], (PACKS, SEQ_LEN, D), 1.0, 6.0, ((0, 4), (1, 8)), (1, 2, 8, 2.0)),
    }


epsilon = 1e-06
soft_cap = 50.0
rope_base = 10000.0
gelu_coef = 0.044715
root_two_pi = 0.7978845608028654

def rounded(tensor):
    return lax.optimization_barrier(tensor.astype(jnp.bfloat16)).astype(jnp.float32)

def inv_rms(tensor):
    return lax.rsqrt(lax.optimization_barrier(jnp.mean(tensor * tensor, axis=-1, keepdims=True)) + epsilon)

def norm_apply(tensor, gain_vec):
    return tensor * inv_rms(tensor) * (1.0 + gain_vec.astype(jnp.float32))

def norm_back(grad_out, tensor, gain_vec):
    scale_val = inv_rms(tensor)
    unit_vec = tensor * scale_val
    weighted = grad_out * (1.0 + gain_vec.astype(jnp.float32))
    grad_in = scale_val * (weighted - unit_vec * lax.optimization_barrier(jnp.mean(weighted * unit_vec, axis=-1, keepdims=True)))
    return (grad_in, lax.optimization_barrier(jnp.sum(grad_out * unit_vec, axis=0)))

def angles(length):
    half_dim = HEAD_DIM // 2
    frequency = jnp.power(rope_base, -(jnp.arange(half_dim, dtype=jnp.float32) * 2.0 / HEAD_DIM))
    angle_grid = jnp.arange(length, dtype=jnp.int32).astype(jnp.float32)[:, None] * frequency[None, :]
    return (jnp.cos(angle_grid)[:, None, :], jnp.sin(angle_grid)[:, None, :])

def rotate(tensor, cosine, sine_part):
    half_dim = tensor.shape[-1] // 2
    first_half = tensor[..., :half_dim]
    second_half = tensor[..., half_dim:]
    return jnp.concatenate([first_half * cosine - second_half * sine_part, second_half * cosine + first_half * sine_part], axis=-1)

def unrotate(tensor, cosine, sine_part):
    half_dim = tensor.shape[-1] // 2
    first_half = tensor[..., :half_dim]
    second_half = tensor[..., half_dim:]
    return jnp.concatenate([first_half * cosine + second_half * sine_part, second_half * cosine - first_half * sine_part], axis=-1)

def gelu_parts(tensor):
    inner = root_two_pi * (tensor + gelu_coef * tensor * tensor * tensor)
    tanh_val = jnp.tanh(inner)
    act_val = 0.5 * tensor * (1.0 + tanh_val)
    slope_val = 0.5 * (1.0 + tanh_val) + 0.5 * tensor * (1.0 - tanh_val * tanh_val) * root_two_pi * (1.0 + 3.0 * gelu_coef * tensor * tensor)
    return (act_val, slope_val)

def visible(query_pos, query_doc, key_pos, key_doc, window):
    same_doc = query_doc[:, None] == key_doc[None, :]
    causal = key_pos[None, :] <= query_pos[:, None]
    inside = query_pos[:, None] - key_pos[None, :] < window
    return same_doc & causal & inside

def trans_dot(left, right):
    return lax.dot_general(left, right, (((0,), (0,)), ((), ())), preferred_element_type=jnp.float32)

def right_dot(left, right):
    return lax.dot_general(left, right, (((1,), (1,)), ((), ())), preferred_element_type=jnp.float32)

def attention_forward(queries, keys_rot, values, doc_local, window):
    length = queries.shape[0]
    block_len = min(512, length)
    block_count = length // block_len
    key_pos = jnp.arange(length, dtype=jnp.int32)

    def query_step(carried, block_index):
        offset = block_index * block_len
        query_blk = lax.dynamic_slice_in_dim(queries, offset, block_len, 0)
        query_pos = offset + jnp.arange(block_len, dtype=jnp.int32)
        query_doc = lax.dynamic_slice_in_dim(doc_local, offset, block_len, 0)
        raw_scores = jnp.einsum('bgrd,kgd->grbk', query_blk.astype(jnp.float32), keys_rot.astype(jnp.float32))
        capped = soft_cap * jnp.tanh(raw_scores / soft_cap)
        allowed = visible(query_pos, query_doc, key_pos, doc_local, window)
        expo_val = jnp.where(allowed, jnp.exp(capped), 0.0)
        totals = lax.optimization_barrier(jnp.sum(expo_val, axis=-1))
        numerator = jnp.einsum('grbk,kgd->bgrd', rounded(expo_val), values.astype(jnp.float32))
        out_blk = numerator / jnp.transpose(totals, (2, 0, 1))[..., None]
        return (carried, (out_blk, totals))
    _, (out_blocks, total_blocks) = lax.scan(query_step, jnp.zeros((), jnp.float32), jnp.arange(block_count, dtype=jnp.int32))
    out32 = out_blocks.reshape((length,) + queries.shape[1:])
    totals = jnp.transpose(total_blocks, (1, 2, 0, 3)).reshape(queries.shape[1], queries.shape[2], length)
    return (out32, totals)

def attention_backward(queries, keys_rot, values, doc_local, window, out32, totals, grad_heads):
    length = queries.shape[0]
    block_len = min(512, length)
    block_count = length // block_len
    key_pos = jnp.arange(length, dtype=jnp.int32)
    delta_sum = lax.optimization_barrier(jnp.sum(grad_heads.astype(jnp.float32) * out32, axis=-1))
    keys_f = keys_rot.astype(jnp.float32)
    values_f = values.astype(jnp.float32)

    def query_step(carried, block_index):
        grad_keys, grad_values = carried
        offset = block_index * block_len
        query_blk = lax.dynamic_slice_in_dim(queries, offset, block_len, 0).astype(jnp.float32)
        grad_blk = lax.dynamic_slice_in_dim(grad_heads, offset, block_len, 0).astype(jnp.float32)
        delta_blk = jnp.transpose(lax.dynamic_slice_in_dim(delta_sum, offset, block_len, 0), (1, 2, 0))
        total_blk = lax.dynamic_slice_in_dim(totals, offset, block_len, 2)
        query_pos = offset + jnp.arange(block_len, dtype=jnp.int32)
        query_doc = lax.dynamic_slice_in_dim(doc_local, offset, block_len, 0)
        raw_scores = jnp.einsum('bgrd,kgd->grbk', query_blk, keys_f)
        capped = soft_cap * jnp.tanh(raw_scores / soft_cap)
        allowed = visible(query_pos, query_doc, key_pos, doc_local, window)
        prob_val = jnp.where(allowed, jnp.exp(capped) / total_blk[..., None], 0.0)
        grad_prob = jnp.einsum('bgrd,kgd->grbk', grad_blk, values_f)
        cap_ratio = capped / soft_cap
        grad_raw = rounded(prob_val * (grad_prob - delta_blk[..., None]) * (1.0 - cap_ratio * cap_ratio))
        grad_query = jnp.einsum('grbk,kgd->bgrd', grad_raw, keys_f)
        grad_keys = grad_keys + jnp.einsum('grbk,bgrd->kgd', grad_raw, query_blk)
        grad_values = grad_values + jnp.einsum('grbk,bgrd->kgd', rounded(prob_val), grad_blk)
        return ((grad_keys, grad_values), grad_query)
    zero_kv = jnp.zeros(keys_rot.shape, jnp.float32)
    (grad_keys, grad_values), grad_blocks = lax.scan(query_step, (zero_kv, zero_kv), jnp.arange(block_count, dtype=jnp.int32))
    return (grad_blocks.reshape(queries.shape), grad_keys, grad_values)

def one_pack(hidden_in, qkv_weights, out_weights, gate_up_weights, down_weights, norm_gains, doc_local, cotangent):
    length = hidden_in.shape[0]
    window = length // 2
    groups = HEADS // KV_HEADS
    query_cols = HEADS * HEAD_DIM
    kv_cols = KV_HEADS * HEAD_DIM
    query_scale = HEAD_DIM ** (-0.5)
    cosine, sine_part = angles(length)
    resid_in = hidden_in.astype(jnp.float32)
    normed_one = norm_apply(resid_in, norm_gains[0]).astype(jnp.bfloat16)
    qkv = jnp.dot(normed_one, qkv_weights, preferred_element_type=jnp.float32)
    queries = (rotate(qkv[:, :query_cols].reshape(length, HEADS, HEAD_DIM), cosine, sine_part) * query_scale).astype(jnp.bfloat16)
    queries = queries.reshape(length, KV_HEADS, groups, HEAD_DIM)
    keys_rot = rotate(qkv[:, query_cols:query_cols + kv_cols].reshape(length, KV_HEADS, HEAD_DIM), cosine, sine_part).astype(jnp.bfloat16)
    values = qkv[:, query_cols + kv_cols:].reshape(length, KV_HEADS, HEAD_DIM).astype(jnp.bfloat16)
    out32, totals = attention_forward(queries, keys_rot, values, doc_local, window)
    out_bf = out32.reshape(length, query_cols).astype(jnp.bfloat16)
    attn_out = right_dot(out_bf, out_weights)
    mid_state = resid_in + norm_apply(attn_out, norm_gains[1])
    normed_two = norm_apply(mid_state, norm_gains[2]).astype(jnp.bfloat16)
    gate_up = jnp.dot(normed_two, gate_up_weights, preferred_element_type=jnp.float32)
    gate_val = gate_up[:, :FF]
    up_val = gate_up[:, FF:]
    act_val, slope_val = gelu_parts(gate_val)
    hidden = (act_val * up_val).astype(jnp.bfloat16)
    ffn_out = right_dot(hidden, down_weights)
    result = (mid_state + norm_apply(ffn_out, norm_gains[3])).astype(jnp.bfloat16)
    grad_top = cotangent.astype(jnp.float32)
    grad_ffn, gain_three = norm_back(grad_top, ffn_out, norm_gains[3])
    grad_ffn_bf = grad_ffn.astype(jnp.bfloat16)
    grad_hidden = jnp.dot(grad_ffn_bf, down_weights, preferred_element_type=jnp.float32)
    grad_gu = jnp.concatenate([grad_hidden * up_val * slope_val, grad_hidden * act_val], axis=1).astype(jnp.bfloat16)
    grad_normed_two = right_dot(grad_gu, gate_up_weights)
    back_mid, gain_two = norm_back(grad_normed_two, mid_state, norm_gains[2])
    grad_mid = grad_top + back_mid
    grad_attn, gain_one = norm_back(grad_mid, attn_out, norm_gains[1])
    grad_attn_bf = grad_attn.astype(jnp.bfloat16)
    grad_heads = jnp.dot(grad_attn_bf, out_weights, preferred_element_type=jnp.float32).astype(jnp.bfloat16)
    grad_heads = grad_heads.reshape(length, KV_HEADS, groups, HEAD_DIM)
    grad_query, grad_keys, grad_values = attention_backward(queries, keys_rot, values, doc_local, window, out32, totals, grad_heads)
    grad_query = unrotate(grad_query.reshape(length, HEADS, HEAD_DIM) * query_scale, cosine, sine_part)
    grad_keys = unrotate(grad_keys, cosine, sine_part)
    grad_qkv = jnp.concatenate([grad_query.reshape(length, query_cols), grad_keys.reshape(length, kv_cols), grad_values.reshape(length, kv_cols)], axis=1).astype(jnp.bfloat16)
    grad_normed_one = right_dot(grad_qkv, qkv_weights)
    back_in, gain_zero = norm_back(grad_normed_one, resid_in, norm_gains[0])
    grad_input = grad_mid + back_in
    return (result, grad_input, trans_dot(normed_one, grad_qkv), trans_dot(grad_attn_bf, out_bf), trans_dot(normed_two, grad_gu), trans_dot(grad_ffn_bf, hidden), jnp.stack([gain_zero, gain_one, gain_two, gain_three], axis=0))

def reference(hidden_in, qkv_weights, out_weights, gate_up_weights, down_weights, norm_gains, doc_ids, cotangent):
    outputs = []
    input_grads = []
    grad_qkv = jnp.zeros(qkv_weights.shape, jnp.float32)
    grad_out = jnp.zeros(out_weights.shape, jnp.float32)
    grad_gu = jnp.zeros(gate_up_weights.shape, jnp.float32)
    grad_down = jnp.zeros(down_weights.shape, jnp.float32)
    grad_gain = jnp.zeros(norm_gains.shape, jnp.float32)
    for pack_index in range(PACKS):
        results = one_pack(hidden_in[pack_index], qkv_weights, out_weights, gate_up_weights, down_weights, norm_gains, doc_ids[pack_index], cotangent[pack_index])
        outputs.append(results[0])
        input_grads.append(results[1])
        grad_qkv = grad_qkv + results[2]
        grad_out = grad_out + results[3]
        grad_gu = grad_gu + results[4]
        grad_down = grad_down + results[5]
        grad_gain = grad_gain + results[6]
    return (jnp.stack(outputs), jnp.stack(input_grads), grad_qkv, grad_out, grad_gu, grad_down, grad_gain)
```

```python
import math

import jax
import jax.numpy as jnp
from jax import lax
from jax.experimental import pallas as pl
from jax.experimental.pallas import tpu as pltpu
from jax.sharding import Mesh
from jax.sharding import PartitionSpec as P

HEADS = 8
KV_HEADS = 4
HEAD_DIM = 256


epsilon = 1e-06
soft_cap = 50.0
rope_base = 10000.0
gelu_coef = 0.044715
root_two_pi = 0.7978845608028654


def inv_rms(tensor):
    return lax.rsqrt(jnp.mean(tensor * tensor, axis=-1, keepdims=True) + epsilon)


def norm_apply(tensor, gain_vec):
    return tensor * inv_rms(tensor) * (1.0 + gain_vec.astype(jnp.float32))


def norm_back(grad_out, tensor, gain_vec):
    scale_val = inv_rms(tensor)
    unit_vec = tensor * scale_val
    weighted = grad_out * (1.0 + gain_vec.astype(jnp.float32))
    grad_in = scale_val * (
        weighted - unit_vec * jnp.mean(weighted * unit_vec, axis=-1, keepdims=True)
    )
    return (grad_in, jnp.sum(grad_out * unit_vec, axis=0))


def rotate(tensor, cosine, sine_part):
    half_dim = tensor.shape[-1] // 2
    first_half = tensor[..., :half_dim]
    second_half = tensor[..., half_dim:]
    return jnp.concatenate(
        [
            first_half * cosine - second_half * sine_part,
            second_half * cosine + first_half * sine_part,
        ],
        axis=-1,
    )


def unrotate(tensor, cosine, sine_part):
    half_dim = tensor.shape[-1] // 2
    first_half = tensor[..., :half_dim]
    second_half = tensor[..., half_dim:]
    return jnp.concatenate(
        [
            first_half * cosine + second_half * sine_part,
            second_half * cosine - first_half * sine_part,
        ],
        axis=-1,
    )


def gelu_parts(tensor):
    inner = root_two_pi * (tensor + gelu_coef * tensor * tensor * tensor)
    tanh_val = jnp.tanh(inner)
    act_val = 0.5 * tensor * (1.0 + tanh_val)
    slope_val = 0.5 * (1.0 + tanh_val) + 0.5 * tensor * (
        1.0 - tanh_val * tanh_val
    ) * root_two_pi * (1.0 + 3.0 * gelu_coef * tensor * tensor)
    return (act_val, slope_val)


def pack_visible(query_pos, query_doc, key_pos, key_doc, window):
    same_doc = jnp.transpose(query_doc)[:, :, None] == jnp.transpose(key_doc)[:, None, :]
    causal = key_pos[None, :] <= query_pos[:, None]
    inside = query_pos[:, None] - key_pos[None, :] < window
    return same_doc & (causal & inside)[None, :, :]


def trans_dot(left, right):
    return lax.dot_general(
        left, right, (((0,), (0,)), ((), ())), preferred_element_type=jnp.float32
    )


def bundle_qkv(matrix, share_count):
    row_total = matrix.shape[0]
    query_part = matrix[:, : HEADS * HEAD_DIM].reshape(row_total, share_count, -1)
    key_part = matrix[:, HEADS * HEAD_DIM : (HEADS + KV_HEADS) * HEAD_DIM].reshape(
        row_total, share_count, -1
    )
    value_part = matrix[:, (HEADS + KV_HEADS) * HEAD_DIM :].reshape(row_total, share_count, -1)
    return jnp.concatenate([query_part, key_part, value_part], axis=2).reshape(row_total, -1)


def unbundle_qkv(matrix, share_count):
    row_total = matrix.shape[0]
    query_width = HEADS * HEAD_DIM // share_count
    key_width = KV_HEADS * HEAD_DIM // share_count
    blocks = matrix.reshape(row_total, share_count, -1)
    return jnp.concatenate(
        [
            blocks[:, :, :query_width].reshape(row_total, -1),
            blocks[:, :, query_width : query_width + key_width].reshape(row_total, -1),
            blocks[:, :, query_width + key_width :].reshape(row_total, -1),
        ],
        axis=1,
    )


def bundle_gate_up(matrix, share_count):
    row_total = matrix.shape[0]
    return jnp.transpose(matrix.reshape(row_total, 2, share_count, -1), (0, 2, 1, 3)).reshape(
        row_total, -1
    )


def unbundle_gate_up(matrix, share_count):
    row_total = matrix.shape[0]
    return jnp.transpose(matrix.reshape(row_total, share_count, 2, -1), (0, 2, 1, 3)).reshape(
        row_total, -1
    )


def widen_rows(matrix):
    return lax.all_gather(matrix[:, None, :], "fsdp", axis=1, tiled=True)


def project_terms(matrix, weight):

    def row_terms(offset, row_count):
        return jnp.einsum("tpc,dc->ptd", matrix, weight, preferred_element_type=jnp.float32)

    return row_terms


def narrow_rows(row_terms):
    return lax.psum_scatter(
        row_terms(jnp.int32(0), 1 * lax.axis_size("fsdp")).astype(jnp.bfloat16),
        "fsdp",
        scatter_dimension=0,
        tiled=True,
    ).astype(jnp.float32)[0]


def on_device(
    hidden_in,
    qkv_weights,
    out_weights,
    gate_up_weights,
    down_weights,
    norm_gains,
    doc_ids,
    cotangent,
):
    resid_bf = hidden_in[0]
    doc_local = doc_ids[0]
    tokens = resid_bf.shape[0]
    model_width = resid_bf.shape[1]
    seq_count = lax.axis_size("seq")
    length = tokens * seq_count
    window = length // 2
    groups = HEADS // KV_HEADS
    query_scale = HEAD_DIM ** (-0.5)
    first_row = lax.axis_index("seq") * tokens
    positions = first_row + jnp.arange(tokens, dtype=jnp.int32)
    half_dim = HEAD_DIM // 2
    frequency = jnp.power(rope_base, -(jnp.arange(half_dim, dtype=jnp.float32) * 2.0 / HEAD_DIM))
    angle_grid = positions.astype(jnp.float32)[:, None] * frequency[None, :]
    cosine = jnp.cos(angle_grid)[:, None, None, :]
    sine_part = jnp.sin(angle_grid)[:, None, None, :]
    share_count = lax.axis_size("fsdp")
    gain_tiles = jnp.tile(jnp.transpose(norm_gains), (1, share_count))
    qkv_swap, out_swap, gu_swap, down_swap, gain_swap = (
        lax.all_to_all(
            bundle_qkv(qkv_weights, share_count), "fsdp", split_axis=1, concat_axis=0, tiled=True
        ),
        lax.all_to_all(out_weights, "fsdp", split_axis=1, concat_axis=0, tiled=True),
        lax.all_to_all(
            bundle_gate_up(gate_up_weights, share_count),
            "fsdp",
            split_axis=1,
            concat_axis=0,
            tiled=True,
        ),
        lax.all_to_all(down_weights, "fsdp", split_axis=1, concat_axis=0, tiled=True),
        lax.all_to_all(gain_tiles, "fsdp", split_axis=1, concat_axis=0, tiled=True),
    )
    qkv_full, out_full, gu_full, down_full, gain_cols = (
        lax.all_gather(qkv_swap, "seq", axis=0, tiled=True),
        lax.all_gather(out_swap, "seq", axis=0, tiled=True),
        lax.all_gather(gu_swap, "seq", axis=0, tiled=True),
        lax.all_gather(down_swap, "seq", axis=0, tiled=True),
        lax.all_gather(gain_swap, "seq", axis=0, tiled=True),
    )
    gain_full = jnp.transpose(gain_cols)
    heads_local = HEADS // share_count
    kv_local = KV_HEADS // share_count
    query_cols = heads_local * HEAD_DIM
    kv_cols = kv_local * HEAD_DIM
    resid_in = resid_bf.astype(jnp.float32)
    normed_one = norm_apply(resid_in, gain_full[0]).astype(jnp.bfloat16)
    wide_one, docs_wide = (
        lax.all_gather(normed_one[:, None, :], "fsdp", axis=1, tiled=True),
        lax.all_gather(doc_local[:, None], "fsdp", axis=1, tiled=True),
    )
    pack_count = wide_one.shape[1]
    flat_rows = tokens * pack_count
    flat_one = wide_one.reshape(flat_rows, model_width)
    qkv = jnp.dot(flat_one, qkv_full, preferred_element_type=jnp.float32).reshape(
        tokens, pack_count, -1
    )
    queries = (
        rotate(
            qkv[..., :query_cols].reshape(tokens, pack_count, heads_local, HEAD_DIM),
            cosine,
            sine_part,
        )
        * query_scale
    ).astype(jnp.bfloat16)
    queries = queries.reshape(tokens, pack_count, kv_local, groups, HEAD_DIM)
    keys_rot = rotate(
        qkv[..., query_cols : query_cols + kv_cols].reshape(tokens, pack_count, kv_local, HEAD_DIM),
        cosine,
        sine_part,
    ).astype(jnp.bfloat16)
    values = qkv[..., query_cols + kv_cols :].astype(jnp.bfloat16)
    packed = jnp.concatenate([keys_rot.reshape(tokens, pack_count, kv_cols), values], axis=2)
    kv_piece = lax.all_gather(packed, "seq", axis=0, tiled=True)
    doc_piece = lax.all_gather(docs_wide, "seq", axis=0, tiled=True)
    row_count = kv_piece.shape[0]
    key_pos = jnp.arange(row_count, dtype=jnp.int32)
    keys_blk = kv_piece[..., :kv_cols].reshape(row_count, pack_count, kv_local, HEAD_DIM)
    values_blk = kv_piece[..., kv_cols:].reshape(row_count, pack_count, kv_local, HEAD_DIM)
    raw_scores = jnp.einsum(
        "bpgrd,kpgd->pgrbk", queries, keys_blk, preferred_element_type=jnp.float32
    )
    capped = soft_cap * jnp.tanh(raw_scores / soft_cap)
    allowed = pack_visible(positions, docs_wide, key_pos, doc_piece, window)
    expo_val = jnp.where(allowed[:, None, None], jnp.exp(capped), 0.0)
    numerator = jnp.einsum(
        "pgrbk,kpgd->bpgrd",
        expo_val.astype(jnp.bfloat16),
        values_blk,
        preferred_element_type=jnp.float32,
    )
    numerator, totals = (numerator, jnp.sum(expo_val, axis=-1))
    out32 = numerator / jnp.transpose(totals, (3, 0, 1, 2))[..., None]
    out_bf = out32.reshape(tokens, pack_count, query_cols).astype(jnp.bfloat16)
    attn_out = narrow_rows(project_terms(out_bf, out_full))
    mid_state = resid_in + norm_apply(attn_out, gain_full[1])
    normed_two = norm_apply(mid_state, gain_full[2]).astype(jnp.bfloat16)
    flat_two = widen_rows(normed_two).reshape(flat_rows, model_width)
    gate_up = jnp.dot(flat_two, gu_full, preferred_element_type=jnp.float32)
    ff_local = gate_up.shape[1] // 2
    gate_val = gate_up[:, :ff_local]
    up_val = gate_up[:, ff_local:]
    act_val, slope_val = gelu_parts(gate_val)
    hidden = (act_val * up_val).astype(jnp.bfloat16)
    ffn_out = narrow_rows(project_terms(hidden.reshape(tokens, pack_count, ff_local), down_full))
    result = (mid_state + norm_apply(ffn_out, gain_full[3])).astype(jnp.bfloat16)
    grad_top = cotangent[0].astype(jnp.float32)
    grad_ffn, gain_three = norm_back(grad_top, ffn_out, gain_full[3])
    grad_ffn_bf = grad_ffn.astype(jnp.bfloat16)
    flat_ffn = widen_rows(grad_ffn_bf).reshape(flat_rows, model_width)
    grad_hidden = jnp.dot(flat_ffn, down_full, preferred_element_type=jnp.float32)
    grad_gu = jnp.concatenate(
        [grad_hidden * up_val * slope_val, grad_hidden * act_val], axis=1
    ).astype(jnp.bfloat16)
    grad_normed_two = narrow_rows(
        project_terms(grad_gu.reshape(tokens, pack_count, 2 * ff_local), gu_full)
    )
    back_mid, gain_two = norm_back(grad_normed_two, mid_state, gain_full[2])
    grad_mid = grad_top + back_mid
    grad_attn, gain_one = norm_back(grad_mid, attn_out, gain_full[1])
    grad_attn_bf = grad_attn.astype(jnp.bfloat16)
    flat_attn = widen_rows(grad_attn_bf).reshape(flat_rows, model_width)
    grad_heads = jnp.dot(flat_attn, out_full, preferred_element_type=jnp.float32).astype(
        jnp.bfloat16
    )
    grad_heads = grad_heads.reshape(tokens, pack_count, kv_local, groups, HEAD_DIM)
    delta_sum = jnp.transpose(
        jnp.sum(grad_heads.astype(jnp.float32) * out32, axis=-1), (1, 2, 3, 0)
    )
    all_packed, all_docs = (
        lax.all_gather(packed, "seq", axis=0, tiled=True),
        lax.all_gather(docs_wide, "seq", axis=0, tiled=True),
    )
    per_block = tokens * math.gcd(seq_count, max(1, 512 // tokens))
    block_count = length // per_block

    def key_block(grad_query, block_index):
        key_start = block_index * per_block
        kv_block = lax.dynamic_slice_in_dim(all_packed, key_start, per_block, 0)
        doc_block = lax.dynamic_slice_in_dim(all_docs, key_start, per_block, 0)
        keys_blk = kv_block[..., :kv_cols].reshape(per_block, pack_count, kv_local, HEAD_DIM)
        values_blk = kv_block[..., kv_cols:].reshape(per_block, pack_count, kv_local, HEAD_DIM)
        key_pos = key_start + jnp.arange(per_block, dtype=jnp.int32)
        raw_scores = jnp.einsum(
            "bpgrd,kpgd->pgrbk", queries, keys_blk, preferred_element_type=jnp.float32
        )
        capped = soft_cap * jnp.tanh(raw_scores / soft_cap)
        allowed = pack_visible(positions, docs_wide, key_pos, doc_block, window)
        prob_val = jnp.where(allowed[:, None, None], jnp.exp(capped) / totals[..., None], 0.0)
        grad_prob = jnp.einsum(
            "bpgrd,kpgd->pgrbk", grad_heads, values_blk, preferred_element_type=jnp.float32
        )
        cap_ratio = capped / soft_cap
        grad_raw = (
            prob_val * (grad_prob - delta_sum[..., None]) * (1.0 - cap_ratio * cap_ratio)
        ).astype(jnp.bfloat16)
        updated = grad_query + jnp.einsum(
            "pgrbk,kpgd->bpgrd", grad_raw, keys_blk, preferred_element_type=jnp.float32
        )
        grad_keys = jnp.einsum(
            "pgrbk,bpgrd->kpgd", grad_raw, queries, preferred_element_type=jnp.float32
        )
        grad_values = jnp.einsum(
            "pgrbk,bpgrd->kpgd",
            prob_val.astype(jnp.bfloat16),
            grad_heads,
            preferred_element_type=jnp.float32,
        )
        return (
            updated,
            jnp.concatenate(
                [
                    grad_keys.reshape(per_block, pack_count, kv_cols),
                    grad_values.reshape(per_block, pack_count, kv_cols),
                ],
                axis=2,
            ),
        )

    grad_query, key_terms = lax.scan(
        key_block,
        jnp.zeros((tokens, pack_count, kv_local, groups, HEAD_DIM), jnp.float32),
        jnp.arange(block_count, dtype=jnp.int32),
    )
    key_grads = lax.psum_scatter(
        key_terms.reshape(length, pack_count, 2 * kv_cols).astype(jnp.bfloat16),
        "seq",
        scatter_dimension=0,
        tiled=True,
    ).astype(jnp.float32)
    grad_query = unrotate(
        grad_query.reshape(tokens, pack_count, heads_local, HEAD_DIM) * query_scale,
        cosine,
        sine_part,
    )
    grad_keys = unrotate(
        key_grads[..., :kv_cols].reshape(tokens, pack_count, kv_local, HEAD_DIM), cosine, sine_part
    )
    grad_qkv = jnp.concatenate(
        [
            grad_query.reshape(tokens, pack_count, query_cols),
            grad_keys.reshape(tokens, pack_count, kv_cols),
            key_grads[..., kv_cols:],
        ],
        axis=2,
    ).astype(jnp.bfloat16)
    grad_normed_one = narrow_rows(project_terms(grad_qkv, qkv_full))
    back_in, gain_zero = norm_back(grad_normed_one, resid_in, gain_full[0])
    grad_input = grad_mid + back_in
    flat_qkv = grad_qkv.reshape(flat_rows, -1)
    flat_out = out_bf.reshape(flat_rows, -1)
    gain_terms = jnp.stack([gain_zero, gain_one, gain_two, gain_three], axis=1)
    edge_one = flat_qkv.shape[1]
    edge_two = edge_one + flat_out.shape[1]
    edge_three = edge_two + grad_gu.shape[1]
    edge_four = edge_three + hidden.shape[1]
    all_terms = jnp.concatenate(
        [
            trans_dot(flat_one, flat_qkv),
            trans_dot(flat_attn, flat_out),
            trans_dot(flat_two, grad_gu),
            trans_dot(flat_ffn, hidden),
            gain_terms,
        ],
        axis=1,
    )
    summed = lax.psum_scatter(
        all_terms.astype(jnp.bfloat16), "seq", scatter_dimension=0, tiled=True
    ).astype(jnp.float32)
    qkv_back, out_back, gu_back, down_back, gain_back = (
        lax.all_to_all(
            summed[:, :edge_one].astype(jnp.bfloat16),
            "fsdp",
            split_axis=0,
            concat_axis=1,
            tiled=True,
        ).astype(jnp.float32),
        lax.all_to_all(
            summed[:, edge_one:edge_two].astype(jnp.bfloat16),
            "fsdp",
            split_axis=0,
            concat_axis=1,
            tiled=True,
        ).astype(jnp.float32),
        lax.all_to_all(
            summed[:, edge_two:edge_three].astype(jnp.bfloat16),
            "fsdp",
            split_axis=0,
            concat_axis=1,
            tiled=True,
        ).astype(jnp.float32),
        lax.all_to_all(
            summed[:, edge_three:edge_four].astype(jnp.bfloat16),
            "fsdp",
            split_axis=0,
            concat_axis=1,
            tiled=True,
        ).astype(jnp.float32),
        lax.all_to_all(
            summed[:, edge_four:].astype(jnp.bfloat16),
            "fsdp",
            split_axis=0,
            concat_axis=1,
            tiled=True,
        ).astype(jnp.float32),
    )
    row_total = qkv_back.shape[0]
    gain_grad = jnp.transpose(jnp.sum(gain_back.reshape(row_total, share_count, 4), axis=1))
    outputs = (
        result[None],
        grad_input[None],
        unbundle_qkv(qkv_back, share_count),
        out_back,
        unbundle_gate_up(gu_back, share_count),
        down_back,
        gain_grad,
    )
    return outputs


CHIPS = 4
RING = 4


def core_swap(array):
    return lax.ppermute(array, "core", [(0, 1), (1, 0)])


def z_shift(array, step):
    return lax.ppermute(array, "z", [(i, (i + step) % RING) for i in range(RING)])


def chip_swap(array, flip):
    return lax.ppermute(array, "chip", [(i, i ^ flip) for i in range(CHIPS)])


def pick(array, index, axis):
    return lax.dynamic_index_in_dim(array, index, axis, keepdims=False)


def put(whole, piece, index, axis):
    return lax.dynamic_update_index_in_dim(whole, piece, index, axis)


def columns_at(matrix, index, count):
    return lax.dynamic_slice_in_dim(matrix, index * count, count, matrix.ndim - 1)


def by_core(core, mine, other, axis):
    first = jnp.where(core == 0, mine, other)
    second = jnp.where(core == 0, other, mine)
    return jnp.stack([first, second], axis=axis)


def back_dot(left, right):
    return lax.dot_general(
        left, right, (((1,), (1,)), ((), ())), preferred_element_type=jnp.float32
    )


def plain_dot(left, right):
    return jnp.dot(left, right, preferred_element_type=jnp.float32)


def soft_scores(query_blk, key_blk):
    return jnp.tanh(back_dot(query_blk, key_blk) * (1.0 / soft_cap))


def attend_kernel(
    place_ref, query_ref, key_ref, value_ref, row_ref, low_ref, col_ref, out_ref, bf_ref, total_ref, acc_ref, sum_ref
):
    chip = place_ref[0]
    blk = query_ref.shape[0] // CHIPS

    def one_block(index, carried):
        rows = pl.ds(pl.multiple_of(index * blk, blk), blk)
        natural = jnp.bitwise_xor(index, chip)
        query_blk = query_ref[rows, :]
        row_pos = row_ref[rows, :]
        row_low = low_ref[rows, :]
        acc_ref[...] = jnp.zeros_like(acc_ref)
        sum_ref[...] = jnp.zeros_like(sum_ref)
        for back in range(3):

            @pl.when(natural >= back)
            def _():
                at = jnp.bitwise_xor(natural - back, chip)
                cols = pl.ds(pl.multiple_of(at * blk, blk), blk)
                ratio = soft_scores(query_blk, key_ref[cols, :])
                col_pos = col_ref[:, cols]
                allowed = (col_pos >= row_low) & (col_pos <= row_pos)
                expo = jnp.where(allowed, jnp.exp(soft_cap * ratio), 0.0)
                sum_ref[...] += jnp.sum(expo, axis=1, keepdims=True)
                acc_ref[...] += plain_dot(expo.astype(jnp.bfloat16), value_ref[cols, :])

        out_val = acc_ref[...] / sum_ref[...]
        out_ref[rows, :] = out_val
        bf_ref[rows, :] = out_val.astype(jnp.bfloat16)
        total_ref[rows, :] = sum_ref[...]
        return carried

    lax.fori_loop(0, CHIPS, one_block, 0)


def attend_back_kernel(
    place_ref,
    query_ref,
    key_ref,
    value_ref,
    row_ref,
    low_ref,
    col_ref,
    out_ref,
    total_ref,
    head_ref,
    dq_ref,
    dk_ref,
    dv_ref,
    acc_ref,
):
    chip = place_ref[0]
    blk = query_ref.shape[0] // CHIPS
    dk_ref[...] = jnp.zeros_like(dk_ref)
    dv_ref[...] = jnp.zeros_like(dv_ref)

    def one_block(index, carried):
        rows = pl.ds(pl.multiple_of(index * blk, blk), blk)
        natural = jnp.bitwise_xor(index, chip)
        query_blk = query_ref[rows, :]
        head_blk = head_ref[rows, :]
        row_pos = row_ref[rows, :]
        row_low = low_ref[rows, :]
        inverse = 1.0 / total_ref[rows, :]
        delta = jnp.sum(head_blk.astype(jnp.float32) * out_ref[rows, :], axis=1, keepdims=True)
        acc_ref[...] = jnp.zeros_like(acc_ref)
        for back in range(3):

            @pl.when(natural >= back)
            def _():
                at = jnp.bitwise_xor(natural - back, chip)
                cols = pl.ds(pl.multiple_of(at * blk, blk), blk)
                key_blk = key_ref[cols, :]
                ratio = soft_scores(query_blk, key_blk)
                col_pos = col_ref[:, cols]
                allowed = (col_pos >= row_low) & (col_pos <= row_pos)
                prob = jnp.where(allowed, jnp.exp(soft_cap * ratio) * inverse, 0.0)
                grad_prob = back_dot(head_blk, value_ref[cols, :])
                grad_raw = (prob * (grad_prob - delta) * (1.0 - ratio * ratio)).astype(jnp.bfloat16)
                acc_ref[...] += plain_dot(grad_raw, key_blk)
                dk_ref[cols, :] += trans_dot(grad_raw, query_blk)
                dv_ref[cols, :] += trans_dot(prob.astype(jnp.bfloat16), head_blk)

        dq_ref[rows, :] = acc_ref[...]
        return carried

    lax.fori_loop(0, CHIPS, one_block, 0)


def local_call(kernel, count, shapes, scratch, flops):
    return pl.pallas_call(
        kernel,
        out_shape=shapes,
        in_specs=[pl.BlockSpec(memory_space=pltpu.SMEM)]
        + [pl.BlockSpec(memory_space=pltpu.VMEM)] * (count - 1),
        out_specs=[pl.BlockSpec(memory_space=pltpu.VMEM)] * len(shapes),
        scratch_shapes=scratch,
        cost_estimate=pl.CostEstimate(
            flops=flops, bytes_accessed=8 * 1024 * 1024, transcendentals=2 * 1024 * 1024
        ),
    )


def gather_pack(block):
    own = jnp.stack([block] + [chip_swap(block, flip) for flip in range(1, CHIPS)])
    return jnp.stack([own, core_swap(own)], axis=1)


def scatter_pack(left, right):
    width = left.shape[-1]
    tokens = left.shape[2]
    other = back_dot(left[:, 1].reshape(-1, width), right).astype(jnp.bfloat16)
    swapped = core_swap(other)
    mine = back_dot(left[:, 0].reshape(-1, width), right) + swapped.astype(jnp.float32)
    mine = mine.reshape(CHIPS, tokens, -1)
    total = mine[0]
    sent = mine.astype(jnp.bfloat16)
    for flip in range(1, CHIPS):
        total = total + chip_swap(sent[flip], flip).astype(jnp.float32)
    return total


def ring_pieces(block):
    pieces = []
    for step in range(RING):
        pieces.append(jnp.concatenate([block, core_swap(block)], axis=0))
        if step < RING - 1:
            block = z_shift(block, 1)
    return pieces


def send_back(partial, step):
    tokens = partial.shape[0] // 2
    swapped = core_swap(partial[tokens:].astype(jnp.bfloat16))
    mine = partial[:tokens] + swapped.astype(jnp.float32)
    if step == 0:
        return mine
    return z_shift(mine.astype(jnp.bfloat16), -step).astype(jnp.float32)


def hidden_columns(matrix, core, plane):
    rows, total = matrix.shape
    mine = columns_at(matrix, core, total // 2)
    other = core_swap(columns_at(matrix, 1 - core, total // 2))
    both = by_core(core, mine, other, 0)
    units = total // 2 // RING
    whole = jnp.zeros((2, RING, rows, units), matrix.dtype)
    for step in range(RING):
        piece = columns_at(both, lax.rem(plane + step, RING), units)
        if step:
            piece = z_shift(piece, step)
        whole = put(whole, piece, lax.rem(plane - step + RING, RING), 1)
    return whole.reshape(2 * RING * rows, units)


def hidden_rows(summed, core, plane):
    units = summed.shape[1]
    blocks = summed.reshape(2, RING, -1, units)
    rows = blocks.shape[2]
    whole = jnp.zeros((2, RING, rows, units), summed.dtype)
    for step in range(RING):
        piece = pick(blocks, lax.rem(plane + step, RING), 1)
        if step:
            piece = z_shift(piece, step)
        whole = put(whole, piece, lax.rem(plane - step + RING, RING), 1)
    mine = pick(whole, core, 0)
    other = core_swap(pick(whole, 1 - core, 0))
    both = by_core(core, mine, other, 0).astype(jnp.float32)
    return jnp.concatenate([both[c, f] for c in range(2) for f in range(RING)], axis=1)


def head_columns(qkv_weights, out_weights, core, chip):
    rows = qkv_weights.shape[0]

    def chunks(which):
        parts = []
        for at in range(CHIPS):
            head, pair = 2 * at + which, HEADS + CHIPS * which + at
            parts.append(
                jnp.concatenate(
                    [
                        columns_at(qkv_weights, head, HEAD_DIM),
                        columns_at(qkv_weights, pair, HEAD_DIM),
                        columns_at(out_weights, head, HEAD_DIM),
                    ],
                    axis=1,
                )
            )
        return jnp.stack(parts)

    mine = chunks(core)
    other = core_swap(chunks(1 - core))
    both = by_core(core, mine, other, 1)
    whole = jnp.zeros_like(both)
    for flip in range(CHIPS):
        at = jnp.bitwise_xor(chip, flip)
        piece = pick(both, at, 0)
        if flip:
            piece = chip_swap(piece, flip)
        whole = put(whole, piece, at, 0)
    return whole.reshape(2 * CHIPS, rows, 3 * HEAD_DIM)


def head_rows(summed, core, chip):
    blocks = summed.reshape((CHIPS, 2) + summed.shape[1:])
    whole = jnp.zeros_like(blocks)
    for flip in range(CHIPS):
        at = jnp.bitwise_xor(chip, flip)
        piece = pick(blocks, at, 0)
        if flip:
            piece = chip_swap(piece, flip)
        whole = put(whole, piece, at, 0)
    mine = pick(whole, core, 1)
    other = core_swap(pick(whole, 1 - core, 1))
    return by_core(core, mine, other, 1)


def ring_rows(blocks, plane):
    seq, rows, width = blocks.shape
    whole = jnp.zeros((seq, RING, rows, width), blocks.dtype)
    for step in range(RING):
        whole = put(whole, blocks, lax.rem(plane - step + RING, RING), 1)
        if step < RING - 1:
            blocks = z_shift(blocks, 1)
    return whole.reshape(seq * RING * rows, width)


def plane_sum(terms, plane):
    width = terms.shape[1]
    blocks = terms.reshape(2 * CHIPS, RING, -1, width)
    total = pick(blocks, plane, 1).astype(jnp.float32)
    for step in range(1, RING):
        piece = pick(blocks, lax.rem(plane + step, RING), 1)
        total = total + z_shift(piece, step).astype(jnp.float32)
    return total.astype(jnp.bfloat16)


def gather_small(block, core, chip, plane):
    planes = jnp.stack([block] + [z_shift(block, step) for step in range(1, RING)])
    planes = jnp.roll(planes[::-1], plane + 1, axis=0)
    chips = jnp.stack([planes] + [chip_swap(planes, flip) for flip in range(1, CHIPS)])
    low = jnp.bitwise_and(chip, 1) == 1
    chips = jnp.where(low, jnp.stack([chips[1], chips[0], chips[3], chips[2]]), chips)
    chips = jnp.where(chip >= 2, jnp.stack([chips[2], chips[3], chips[0], chips[1]]), chips)
    return by_core(core, chips, core_swap(chips), 1)


def sum_small(terms, core, chip, plane):
    for swap in (core_swap, lambda a: chip_swap(a, 1), lambda a: chip_swap(a, 2)):
        terms = terms + swap(terms)
    own = pick(terms, 2 * chip + core, 0)
    total = pick(own, plane, 0)
    for step in range(1, RING):
        total = total + z_shift(pick(own, lax.rem(plane + step, RING), 0), step)
    return total


def fast_device(
    hidden_in,
    qkv_weights,
    out_weights,
    gate_up_weights,
    down_weights,
    norm_gains,
    doc_ids,
    cotangent,
):
    chip = lax.axis_index("chip").astype(jnp.int32)
    core = lax.axis_index("core").astype(jnp.int32)
    plane = lax.axis_index("z").astype(jnp.int32)
    resid_bf = hidden_in[0]
    tokens, width = resid_bf.shape
    length = 2 * CHIPS * tokens
    window = length // 2
    rows = qkv_weights.shape[0]
    half_dim = HEAD_DIM // 2
    query_scale = HEAD_DIM ** (-0.5)
    ff_width = down_weights.shape[1]
    bf = jnp.bfloat16

    small = jnp.concatenate(
        [jnp.pad(norm_gains, ((0, 0), (0, tokens - rows))), doc_ids.astype(bf), jnp.zeros((3, tokens), bf)], axis=0
    )
    small_all = gather_small(small, core, chip, plane)
    gain_full = jnp.transpose(small_all[..., :4, :rows].reshape(-1, 4, rows), (1, 0, 2)).reshape(4, width)
    doc_all = pick(small_all, plane, 2)[:, :, 4].astype(jnp.int32)
    below_one = jnp.sum((doc_all < 1).astype(jnp.int32))
    below_two = jnp.sum((doc_all < 2).astype(jnp.int32))

    pack_rel = gather_pack(resid_bf)
    head_cols = head_columns(qkv_weights, out_weights, core, chip)
    qkv_own = ring_rows(head_cols[:, :, : 2 * HEAD_DIM], plane)
    out_own = ring_rows(head_cols[:, :, 2 * HEAD_DIM :], plane)
    gate_own = lax.all_gather(
        hidden_columns(gate_up_weights[:, :ff_width], core, plane), "chip", axis=0, tiled=True
    )
    up_own = lax.all_gather(
        hidden_columns(gate_up_weights[:, ff_width:], core, plane), "chip", axis=0, tiled=True
    )
    down_own = lax.all_gather(
        hidden_columns(down_weights, core, plane), "chip", axis=0, tiled=True
    )

    flips = jnp.arange(CHIPS, dtype=jnp.int32)
    block_of = (
        2 * jnp.bitwise_xor(chip, flips)[:, None]
        + jnp.bitwise_xor(core, jnp.arange(2, dtype=jnp.int32))[None, :]
    )
    positions = (
        block_of[:, :, None] * tokens + jnp.arange(tokens, dtype=jnp.int32)[None, None, :]
    ).reshape(length)
    doc_first = jnp.where(positions < below_one, 0, jnp.where(positions < below_two, below_one, below_two))
    lowest = jnp.maximum(doc_first, positions - (window - 1))
    frequency = jnp.power(rope_base, -(jnp.arange(half_dim, dtype=jnp.float32) * 2.0 / HEAD_DIM))
    angle_grid = positions.astype(jnp.float32)[:, None] * frequency[None, :]
    cosine, sine_part = jnp.cos(angle_grid), jnp.sin(angle_grid)
    cosine_kv = jnp.where(core == 0, cosine, 1.0)
    sine_kv = jnp.where(core == 0, sine_part, 0.0)

    resid_in = resid_bf.astype(jnp.float32)
    normed_one = norm_apply(pack_rel.astype(jnp.float32), gain_full[0]).astype(bf)
    normed_one = normed_one.reshape(length, width)

    qkv = plain_dot(normed_one, qkv_own)
    queries = (rotate(qkv[:, :HEAD_DIM], cosine, sine_part) * query_scale).astype(bf)
    kv_mine = rotate(qkv[:, HEAD_DIM:], cosine_kv, sine_kv).astype(bf)

    def swap_tokens(array):
        blocks = array.reshape(CHIPS, 2, tokens, -1)
        flipped = jnp.concatenate([blocks[:, 1:], blocks[:, :1]], axis=1)
        return core_swap(flipped.reshape(length, -1))

    kv_other = swap_tokens(kv_mine)
    keys_rot = jnp.where(core == 0, kv_mine, kv_other)
    values = jnp.where(core == 0, kv_other, kv_mine)
    place = jnp.stack([chip, core])
    row_pos, row_low, col_pos = positions[:, None], lowest[:, None], positions[None, :]
    blk = length // CHIPS
    out32, out_bf, totals = local_call(
        attend_kernel,
        7,
        (
            jax.ShapeDtypeStruct((length, HEAD_DIM), jnp.float32),
            jax.ShapeDtypeStruct((length, HEAD_DIM), bf),
            jax.ShapeDtypeStruct((length, 1), jnp.float32),
        ),
        [pltpu.VMEM((blk, HEAD_DIM), jnp.float32), pltpu.VMEM((blk, 1), jnp.float32)],
        4 * length * length * HEAD_DIM,
    )(place, queries, keys_rot, values, row_pos, row_low, col_pos)
    attn_out = scatter_pack(out_bf.reshape(CHIPS, 2, tokens, HEAD_DIM), out_own)
    mid_state = resid_in + norm_apply(attn_out, gain_full[1])
    normed_two = norm_apply(mid_state, gain_full[2]).astype(bf)

    two_pieces = ring_pieces(normed_two)
    gates, ups, hiddens = [], [], []
    ffn_out = None
    for step in range(RING):
        gate_val = plain_dot(two_pieces[step], gate_own)
        up_val = plain_dot(two_pieces[step], up_own)
        act_val, _ = gelu_parts(gate_val)
        hidden = (act_val * up_val).astype(bf)
        back = send_back(back_dot(hidden, down_own), step)
        ffn_out = back if step == 0 else ffn_out + back
        gates.append(gate_val)
        ups.append(up_val)
        hiddens.append(hidden)
    result = (mid_state + norm_apply(ffn_out, gain_full[3])).astype(bf)
    grad_top = cotangent[0].astype(jnp.float32)
    grad_ffn, gain_three = norm_back(grad_top, ffn_out, gain_full[3])
    ffn_pieces = ring_pieces(grad_ffn.astype(bf))
    grad_gates, grad_ups = [], []
    grad_two = None
    for step in range(RING):
        grad_hidden = plain_dot(ffn_pieces[step], down_own)
        act_val, slope_val = gelu_parts(gates[step])
        grad_gate = (grad_hidden * ups[step] * slope_val).astype(bf)
        grad_up = (grad_hidden * act_val).astype(bf)
        back = send_back(back_dot(grad_gate, gate_own) + back_dot(grad_up, up_own), step)
        grad_two = back if step == 0 else grad_two + back
        grad_gates.append(grad_gate)
        grad_ups.append(grad_up)

    def chip_sum(left, right):
        return lax.psum_scatter(
            trans_dot(left, right).astype(bf), "chip", scatter_dimension=0, tiled=True
        )

    two_all = jnp.concatenate(two_pieces, axis=0)
    down_sum = chip_sum(jnp.concatenate(ffn_pieces, axis=0), jnp.concatenate(hiddens, axis=0))
    gate_sum = chip_sum(two_all, jnp.concatenate(grad_gates, axis=0))
    up_sum = chip_sum(two_all, jnp.concatenate(grad_ups, axis=0))
    down_grad = hidden_rows(down_sum, core, plane)
    gate_grad = hidden_rows(gate_sum, core, plane)
    up_grad = hidden_rows(up_sum, core, plane)

    back_mid, gain_two = norm_back(grad_two, mid_state, gain_full[2])
    grad_mid = grad_top + back_mid
    grad_attn, gain_one = norm_back(grad_mid, attn_out, gain_full[1])
    attn_all = gather_pack(grad_attn.astype(bf)).reshape(length, width)
    grad_heads = plain_dot(attn_all, out_own).astype(bf)
    out_sum = plane_sum(trans_dot(attn_all, out_bf).astype(bf), plane)
    whole = jax.ShapeDtypeStruct((length, HEAD_DIM), jnp.float32)
    grad_query, grad_keys, grad_values = local_call(
        attend_back_kernel,
        10,
        (whole, whole, whole),
        [pltpu.VMEM((blk, HEAD_DIM), jnp.float32)],
        10 * length * length * HEAD_DIM,
    )(place, queries, keys_rot, values, row_pos, row_low, col_pos, out32, totals, grad_heads)
    kept = jnp.where(core == 0, grad_keys, grad_values)
    given = jnp.where(core == 0, grad_values, grad_keys)
    grad_kv = unrotate(kept + swap_tokens(given), cosine_kv, sine_kv)
    grad_query = unrotate(grad_query * query_scale, cosine, sine_part)
    grad_qkv = jnp.concatenate([grad_query, grad_kv], axis=1).astype(bf)
    grad_one = scatter_pack(grad_qkv.reshape(CHIPS, 2, tokens, 2 * HEAD_DIM), qkv_own)
    back_in, gain_zero = norm_back(grad_one, resid_in, gain_full[0])
    grad_input = grad_mid + back_in
    qkv_sum = plane_sum(trans_dot(normed_one, grad_qkv).astype(bf), plane)

    heads = head_rows(jnp.concatenate([qkv_sum, out_sum], axis=2), core, chip).astype(jnp.float32)
    in_order = [(at, which) for at in range(CHIPS) for which in range(2)]
    qkv_parts = [heads[at, which, :, :HEAD_DIM] for at, which in in_order]
    qkv_parts += [
        heads[at, which, :, HEAD_DIM : 2 * HEAD_DIM] for which in range(2) for at in range(CHIPS)
    ]
    out_grad = jnp.concatenate(
        [heads[at, which, :, 2 * HEAD_DIM :] for at, which in in_order], axis=1
    )

    gain_terms = jnp.stack([gain_zero, gain_one, gain_two, gain_three], axis=0)
    gain_terms = jnp.transpose(gain_terms.reshape(4, 2 * CHIPS * RING, rows), (1, 0, 2))
    gain_terms = jnp.pad(gain_terms, ((0, 0), (0, 4), (0, tokens - rows)))
    gain_terms = gain_terms.reshape(2 * CHIPS, RING, 8, tokens)
    gain_grad = sum_small(gain_terms, core, chip, plane)[:4, :rows]
    return (
        result[None],
        grad_input[None],
        jnp.concatenate(qkv_parts, axis=1),
        out_grad,
        jnp.concatenate([gate_grad, up_grad], axis=1),
        down_grad,
        gain_grad,
    )


def solution(mesh):
    seq_count, share_count = mesh.shape["seq"], mesh.shape["fsdp"]

    def layer(*arrays):
        packs, length, _ = arrays[0].shape
        if seq_count == HEADS == 2 * CHIPS and share_count == RING == packs:
            body, axes = fast_device, ("chip", "core", "z")
            inner = Mesh(mesh.devices.reshape(CHIPS, 2, RING), axes)
            seq, fsdp, rows = ("chip", "core"), "z", axes
        else:
            body, inner = on_device, mesh
            seq, fsdp, rows = "seq", "fsdp", ("seq", "fsdp")
        tokens = P(fsdp, seq, None)
        weight = P(rows, None)
        gains = P(None, rows)
        return jax.shard_map(
            body,
            mesh=inner,
            in_specs=(tokens, weight, weight, weight, weight, gains, P(fsdp, seq), tokens),
            out_specs=(tokens, tokens, weight, weight, weight, weight, gains),
            check_vma=False,
        )(*arrays)

    return layer
```
